32 devices in a mesh: frag: 8 (over z, x), band: 4 (over y, core).
Axes of the slice: x: 2, y: 2, z: 4, core: 2. Of those that a mesh axis runs over, the one named last changes fastest.
Arguments:
- wave_init: bfloat16 [8, 4, 64, 64, 128], P('frag', 'band'), may hold values from -6 to 6
- potential: float32 [256, 128, 128], P('frag', 'band'), may hold values from -4 to 4
- fragment_order: int32 [8, 1], P('frag'), may hold values from 0 to 15, as said below
Outputs:
- density: float32 [256, 128, 128], P('frag', 'band')
The draws below stay inside these ranges and needn't reach their ends.
Inputs may be any that keep to these rules, and one draw needn't show every extreme that they name: `fragment_order`: every group holds at least one code q with (q % 4) // 2 == 1; a group may hold the same code in two slots.
All inputs are finite; a program needn't handle non-finite values.
Results may differ from the reference program's by a relative error of at most 0.0003.
Values sent between devices are 32-bit elements; how exact they have to be, the bound alone decides.
A program may use at most 64 MiB of HBM per device.

```python
import jax
import jax.numpy as jnp
from jax import lax

XC = 128
PZ = 32
PY = 32
FRAG_DEV = 1
FRAGS = 8
NB = 4
NZ = 256
NY = 128
ZMAX = 64
YMAX = 64
N_FRAG = 8
N_BAND = 4


def draw_fragment_order(key, part):
    code_key = jax.random.fold_in(key, 11)
    slot_key = jax.random.fold_in(key, 23)
    codes = jax.random.randint(code_key, (N_FRAG, FRAG_DEV), 0, 4 * N_BAND, dtype=jnp.int32)
    chosen = jax.random.randint(slot_key, (N_FRAG,), 0, FRAG_DEV, dtype=jnp.int32)
    deepened = codes // 4 * 4 + 2 + codes % 2
    group_ids = jnp.arange(N_FRAG, dtype=jnp.int32)
    deepened = jnp.where((group_ids == 0)[:, None], 4 * N_BAND - 1, deepened)
    slot_ids = jnp.arange(FRAG_DEV, dtype=jnp.int32)
    return jnp.where(slot_ids[None, :] == chosen[:, None], deepened, codes).astype(jnp.int32)


def levels(rng, shape, shards, least, largest):
    def one(dim, parts):
        heights = jax.random.uniform(jax.random.fold_in(jax.random.fold_in(rng, 6), dim), (parts,), jnp.float32, least / len(shards), largest / len(shards))
        return jnp.repeat(jnp.exp(heights), shape[dim] // parts).reshape((-1,) + (1,) * (len(shape) - dim - 1))

    level = one(*shards[0])
    for cut in shards[1:]:
        level = level * one(*cut)
    return level


def normal_values(own_key, shape, scale, bound, shards=(), kind=jnp.bfloat16):
    result = jax.random.normal(own_key, shape, jnp.float32) * scale
    if len(shards) > 0:
        result = levels(own_key, shape, shards, -0.22, 0.18) * result
    return jnp.clip(result, min=-bound, max=bound).astype(kind)


def setup_inputs(seed: int = 0) -> dict:
    key_of = jax.random.split(jax.random.key(seed), 4)
    return {
        "wave_init": normal_values(key_of[0], (FRAGS, NB, ZMAX, YMAX, XC), 1.0, 6.0, ((0, 8), (1, 4))),
        "potential": normal_values(key_of[1], (NZ, NY, XC), 1.0, 4.0, ((0, 8), (1, 4)), jnp.float32),
        "fragment_order": draw_fragment_order(jax.random.fold_in(key_of[3], 71), 0),
    }


STEP_LENGTH = 0.1
EPSILON = 1e-06

def kinetic(extent, live_length):
    positions = jnp.arange(live_length, dtype=jnp.int32)
    angles = (positions[:, None] * positions[None, :] % live_length).astype(jnp.float32) * (2.0 * jnp.pi / live_length)
    folded = jnp.minimum(positions, live_length - positions).astype(jnp.float32)
    weight = (2.0 * jnp.pi * folded / live_length) ** 2
    cosine = jnp.cos(angles)
    sine = jnp.sin(angles)
    matrix = jnp.dot(cosine * weight[None, :], cosine.T, precision=lax.Precision.HIGHEST)
    matrix = matrix + jnp.dot(sine * weight[None, :], sine.T, precision=lax.Precision.HIGHEST)
    matrix = matrix / live_length
    return jnp.pad(matrix, ((0, extent - live_length), (0, extent - live_length)))

def geometry(slot_ids, columns, box_depth, box_width, length):
    piece_column = slot_ids // 4
    z_double = slot_ids % 4 // 2
    y_double = slot_ids % 2
    column_ids = jnp.arange(columns, dtype=jnp.int32)
    lower_pick = (piece_column[:, None] == column_ids[None, :]).astype(jnp.float32)
    upper_pick = (((piece_column + 1) % columns)[:, None] == column_ids[None, :]).astype(jnp.float32)
    z_lines = jnp.arange(box_depth, dtype=jnp.int32)
    y_lines = jnp.arange(box_width, dtype=jnp.int32)
    live_z = z_lines[None, :] < (box_depth // 2 * (1 + z_double))[:, None]
    live_y = y_lines[None, :] < (box_width // 2 * (1 + y_double))[:, None]
    live_mask = (live_z[:, :, None] & live_y[:, None, :]).astype(jnp.float32)[..., None]
    box_cells = (box_depth // 2 * (1 + z_double) * (box_width // 2) * (1 + y_double) * length).astype(jnp.float32)
    fragment_sign = jnp.where(z_double == y_double, 1.0, -1.0).astype(jnp.float32)
    z_ops = jnp.where((z_double == 1)[:, None, None], kinetic(box_depth, box_depth)[None], kinetic(box_depth, box_depth // 2)[None])
    y_ops = jnp.where((y_double == 1)[:, None, None], kinetic(box_width, box_width)[None], kinetic(box_width, box_width // 2)[None])
    return (lower_pick, upper_pick, live_mask, box_cells, fragment_sign, z_ops, y_ops)

def hamiltonian(states, box_potential, live_mask, x_op, z_ops, y_ops):
    spectral = jnp.einsum('sbzyx,xw->sbzyw', states, x_op, precision=lax.Precision.HIGHEST)
    spectral = spectral + jnp.einsum('sbzyx,szw->sbwyx', states, z_ops, precision=lax.Precision.HIGHEST)
    spectral = spectral + jnp.einsum('sbzyx,syw->sbzwx', states, y_ops, precision=lax.Precision.HIGHEST)
    applied = 0.5 * spectral + box_potential[:, None] * states
    return applied * live_mask[:, None]

def gradient_step(states, box_potential, live_mask, box_cells, x_op, z_ops, y_ops):
    applied = hamiltonian(states, box_potential, live_mask, x_op, z_ops, y_ops)
    intersection = lax.optimization_barrier(jnp.sum(states * states, axis=(2, 3, 4))) + EPSILON
    rayleigh = lax.optimization_barrier(jnp.sum(states * applied, axis=(2, 3, 4))) / intersection
    stepped = states - STEP_LENGTH * (applied - rayleigh[:, :, None, None, None] * states)
    weight = lax.optimization_barrier(jnp.sum(stepped * stepped, axis=(2, 3, 4))) + EPSILON
    return stepped * jnp.sqrt(box_cells[:, None] / weight)[:, :, None, None, None]

def reference(wave_init, potential, fragment_order):
    x_op = kinetic(XC, XC)
    doubled = jnp.concatenate([potential, potential[:2 * PZ]], axis=0)

    def group_density(group_index):
        slot_ids = lax.dynamic_index_in_dim(fragment_order, group_index, 0, keepdims=False)
        lower_pick, upper_pick, live_mask, box_cells, fragment_sign, z_ops, y_ops = geometry(slot_ids, N_BAND, ZMAX, YMAX, XC)
        region = lax.dynamic_slice_in_dim(doubled, group_index * PZ, 2 * PZ, 0)
        region_cols = region.reshape(2 * PZ, N_BAND, PY, XC)
        lower_box = jnp.einsum('sp,zpqx->szqx', lower_pick, region_cols, precision=lax.Precision.HIGHEST)
        upper_box = jnp.einsum('sp,zpqx->szqx', upper_pick, region_cols, precision=lax.Precision.HIGHEST)
        box_potential = jnp.concatenate([lower_box, upper_box], axis=2)
        states = lax.dynamic_slice_in_dim(wave_init, group_index * FRAG_DEV, FRAG_DEV, 0).astype(jnp.float32)
        states = states * live_mask[:, None]
        for repeat in range(2):
            states = gradient_step(states, box_potential, live_mask, box_cells, x_op, z_ops, y_ops)
        box_density = fragment_sign[:, None, None, None] * lax.optimization_barrier(jnp.sum(states * states, axis=1)) / NB
        placed = jnp.einsum('sp,szqx->zpqx', lower_pick, box_density[:, :, :PY], precision=lax.Precision.HIGHEST)
        placed = placed + jnp.einsum('sp,szqx->zpqx', upper_pick, box_density[:, :, PY:], precision=lax.Precision.HIGHEST)
        return placed.reshape(2 * PZ, NY, XC)
    regions = lax.map(group_density, jnp.arange(N_FRAG, dtype=jnp.int32))
    density = regions[:, :PZ] + jnp.roll(regions[:, PZ:], 1, axis=0)
    return density.reshape(NZ, NY, XC)
```

```python
import functools

import jax
import jax.numpy as jnp
import numpy as np
from jax import lax
from jax.experimental import pallas as pl
from jax.experimental.pallas import tpu as pltpu
from jax.sharding import PartitionSpec as P

STEP_LENGTH = 0.1
EPSILON = 1e-06
MESH = pl.DeviceIdType.MESH
PARTS = 4


def half_kinetic(extent, live_length):
    m = np.arange(live_length)
    weight = (2.0 * np.pi * np.minimum(m, live_length - m) / live_length) ** 2
    gap = m[:, None] - m[None, :]
    matrix = np.einsum(
        "m,mij->ij", weight, np.cos(2.0 * np.pi * (m[:, None, None] * gap[None] % live_length) / live_length)
    )
    full = np.zeros((extent, extent))
    full[:live_length, :live_length] = 0.5 * matrix / live_length
    return full


def two_parts(matrix):
    high = matrix.astype(jnp.bfloat16)
    low = (matrix - high.astype(np.float64)).astype(jnp.bfloat16)
    return high, low


def x_operator(length):
    high, low = two_parts(half_kinetic(length, length))
    return np.block([[high, low], [high, np.zeros_like(high)]]).astype(jnp.bfloat16)


def line_operators(extent):
    rows = []
    for live in (extent // 2, extent):
        high, low = two_parts(half_kinetic(extent, live))
        rows.append(np.concatenate([high, low, high], axis=1))
    return np.stack(rows).astype(jnp.bfloat16)


def fold(block):
    return jnp.sum(block.reshape(-1, 8, block.shape[-1]), axis=0)


def dot(a, b):
    return jnp.dot(a, b, preferred_element_type=jnp.float32)


def split(block):
    high = block.astype(jnp.bfloat16)
    return high, (block - high.astype(jnp.float32)).astype(jnp.bfloat16)


def kernel(
    n_frag, n_band, depth, width, length,
    code_ref, wave_ref, pot_ref, kx_ref, kz_ref, ky_ref, out_ref,
    state, applied, box, columns, picked, mine, before,
    to_pair, from_pair, upper, above, lower, to_chip, from_chip, kept, last, ending,
    code_sem, pair_sem, chip_sem, relay_sem, pick_sem, rise_sem,
    half_sem, up_sem, row_sem, end_sem,
):
    g = lax.axis_index("frag")
    b = lax.axis_index("band")
    core = lax.rem(b, 2)
    chip = lax.div(b, 2)
    chips = n_band // 2
    after_g = lax.rem(g + 1, n_frag)
    before_g = lax.rem(g + n_frag - 1, n_frag)
    pair = (g, chip * 2 + 1 - core)
    others = [lax.rem(chip + d, chips) for d in range(1, chips)]
    sources = [lax.rem(chip + chips - d, chips) for d in range(1, chips)]
    slab = depth // 2
    piece = width // 2
    sent = []

    def send(src, dst, sems, index, device):
        copy = pltpu.make_async_remote_copy(
            src_ref=src, dst_ref=dst, send_sem=sems.at[(0, *index)], recv_sem=sems.at[(1, *index)],
            device_id=device, device_id_type=MESH,
        )
        copy.start()
        sent.append(copy)
        return copy

    code = code_ref[0, 0]
    column = lax.shift_right_logical(code, 2)
    z_double = lax.bitwise_and(lax.shift_right_logical(code, 1), 1)
    y_double = lax.bitwise_and(code, 1)
    mine[...] = jnp.full(mine.shape, code, jnp.int32)

    barrier = pltpu.get_barrier_semaphore()
    peers = [pair, (after_g, b), (before_g, b)] + [(g, 2 * o + core) for o in others]
    for peer in peers:
        pl.semaphore_signal(barrier, inc=1, device_id=peer, device_id_type=MESH)
    pl.semaphore_wait(barrier, len(peers))

    step = slab // PARTS
    code_copy = send(mine, before, code_sem, (0,), (after_g, b))
    pair_copies, chip_copies = [], []
    for c in range(PARTS):
        rows = pl.ds(c * step, step)
        chip_copies.append([
            send(pot_ref.at[rows], columns.at[b, rows], chip_sem, (i, c), (g, 2 * o + core))
            for i, o in enumerate(others)
        ])
        pair_copies.append(send(pot_ref.at[rows], columns.at[b, rows], pair_sem, (c,), pair))
    columns[b] = pot_ref[...]

    y_live = lax.broadcasted_iota(jnp.int32, (width, length), 0) < piece * (1 + y_double)

    def begin(z, carry):
        rows = pl.ds(pl.multiple_of(z * width, width), width)
        live = jnp.logical_and(y_live, z < slab * (1 + z_double))
        state[rows, :] = jnp.where(live, wave_ref[rows, :].astype(jnp.float32), 0.0)
        return carry

    lax.fori_loop(0, depth, begin, 0, unroll=4)

    def along_z(first, count, exact):
        op = kz_ref[z_double]
        op = op[:, : 2 * depth] if exact else op

        def one(i, carry):
            y = first + 2 * i
            parts = []
            for e in range(2):
                block = state[pl.ds(y + e, depth, stride=width), :]
                if exact:
                    high = block.astype(jnp.bfloat16)
                    parts.append(jnp.concatenate([high, high], axis=0))
                else:
                    high, low = split(block)
                    parts.append(jnp.concatenate([high, high, low], axis=0))
            result = dot(op, jnp.concatenate(parts, axis=1))
            for e in range(2):
                applied[pl.ds(y + e, depth, stride=width), :] = result[:, e * length : (e + 1) * length]
            return carry

        lax.fori_loop(0, count // 2, one, 0, unroll=4)

    def along_xy(z, exact):
        rows = pl.ds(pl.multiple_of(z * width, 2 * width), 2 * width)
        block = state[rows, :]
        op = ky_ref[y_double]
        if exact:
            high = block.astype(jnp.bfloat16)
            wide = dot(high, kx_ref[0:length, :])
            parts = [jnp.concatenate([high[e * width : (e + 1) * width]] * 2, axis=0) for e in range(2)]
            op = op[:, : 2 * width]
        else:
            high, low = split(block)
            wide = dot(jnp.concatenate([high, low], axis=1), kx_ref[...])
            parts = []
            for e in range(2):
                own = slice(e * width, (e + 1) * width)
                parts.append(jnp.concatenate([high[own], high[own], low[own]], axis=0))
        tall = dot(op, jnp.concatenate(parts, axis=1))
        total = applied[rows, :] + (wide[:, :length] + wide[:, length:])
        total = total + jnp.concatenate([tall[:, :length], tall[:, length:]], axis=0)
        return rows, block, total

    def first_xy(first, count):
        def one(i, carry):
            rows, _, total = along_xy(first + 2 * i, True)
            applied[rows, :] = total
            return carry

        lax.fori_loop(0, count // 2, one, 0, unroll=4)

    picks, rises = [], []

    def relay_columns(c):
        rows = pl.ds(c * step, step)
        relays = []
        for i, s in enumerate(sources):
            chip_copies[c][i].wait_recv()
            here = columns.at[2 * s + core, rows]
            relays.append(send(here, here, relay_sem, (i, c), pair))
        pair_copies[c].wait_recv()
        return relays

    def pick_column(c, relays):
        rows = pl.ds(c * step, step)
        for relay in relays:
            relay.wait_recv()
        if c == 0:
            code_copy.wait_recv()
        target = lax.rem(lax.shift_right_logical(before[0:1, :], 2) + core, n_band)
        value = columns[0, rows]
        for n in range(1, n_band):
            value = jnp.where(jnp.broadcast_to((target == n)[None], value.shape), columns[n, rows], value)
        picked[c] = value
        picks.append(send(
            picked.at[c], box.at[pl.ds(slab + c * step, step), core], pick_sem, (c,), (before_g, b)
        ))

    def pass_up(c):
        picks[c].wait_recv()
        here = box.at[pl.ds(slab + c * step, step), core]
        rises.append(send(here, here, rise_sem, (c,), pair))

    half = width // 2
    along_z(0, half, True)
    relays = relay_columns(0)
    along_z(half, width - half, True)
    pick_column(0, relays)
    relays = relay_columns(1)
    first_xy(0, depth // 2)
    pick_column(1, relays)
    relays = relay_columns(2)
    pass_up(0)
    first_xy(depth // 2, depth // 2)
    pick_column(2, relays)
    relays = relay_columns(3)
    pass_up(1)
    pick_column(3, relays)

    next_column = lax.rem(column + 1, n_band)

    def lower_box(z, carry):
        box[z, 0] = columns[column, z]
        box[z, 1] = columns[next_column, z]
        return carry

    lax.fori_loop(0, slab, lower_box, 0, unroll=4)

    def first_full(first, count, sums):
        def one(i, carry):
            own, cross = carry
            z = first + i
            rows = pl.ds(pl.multiple_of(z * width, width), width)
            s = state[rows, :]
            h = applied[rows, :] + box[z].reshape(width, length) * s
            applied[rows, :] = h
            return own + fold(s * s), cross + fold(s * h)

        return lax.fori_loop(0, count, one, sums, unroll=4)

    zero = jnp.zeros((8, length), jnp.float32)
    sums = first_full(0, slab, (zero, zero))
    pass_up(2)
    pass_up(3)
    for c in range(PARTS):
        rises[c].wait_recv()
        sums = first_full(slab + c * step, step, sums)

    def whole(block):
        return jnp.sum(block, axis=(0, 1), keepdims=True)

    rayleigh = whole(sums[1]) / (whole(sums[0]) + EPSILON)
    gain = 1.0 + STEP_LENGTH * rayleigh

    def advance(z, carry):
        rows = pl.ds(pl.multiple_of(z * width, width), width)
        t = gain * state[rows, :] - STEP_LENGTH * applied[rows, :]
        state[rows, :] = t
        return carry + fold(t * t)

    weight = whole(lax.fori_loop(0, depth, advance, zero, unroll=4))

    along_z(0, width, False)

    def second(i, carry):
        cross, square = carry
        z = 2 * i
        rows, t, total = along_xy(z, False)
        h = total + box[pl.ds(z, 2)].reshape(2 * width, length) * t
        applied[rows, :] = h
        return cross + fold(t * h), square + fold(h * h)

    cross, square = lax.fori_loop(0, depth // 2, second, (zero, zero), unroll=2)
    cross, square = whole(cross), whole(square)

    cells = (slab * piece * length * (1 + z_double) * (1 + y_double)).astype(jnp.float32)
    scale1 = cells / (weight + EPSILON)
    rayleigh = scale1 * cross / (scale1 * weight + EPSILON)
    gain = 1.0 + STEP_LENGTH * rayleigh
    stepped = gain * gain * weight - 2.0 * STEP_LENGTH * gain * cross + STEP_LENGTH * STEP_LENGTH * square
    scale2 = cells / (scale1 * stepped + EPSILON)
    sign = jnp.where(z_double == y_double, 1.0, -1.0).astype(jnp.float32) / n_band
    factor = sign * scale1 * scale2

    share = slab // 2
    lines = share // PARTS

    def density(z):
        rows = pl.ds(pl.multiple_of(z * width, width), lines * width)
        u = gain * state[rows, :] - STEP_LENGTH * applied[rows, :]
        return (factor * (u * u)).reshape(lines, 2, piece, length)

    halves = {}
    def give(level, j):
        to_pair[level, j] = density(level * slab + share * (1 - core) + lines * j)
        halves[level, j] = send(to_pair.at[level, j], from_pair.at[level, j], half_sem, (level, j), pair)

    def take(level, j):
        own = density(level * slab + share * core + lines * j)
        halves[level, j].wait_recv()
        return own + from_pair[level, j]

    ups = []
    give(1, 0)
    for j in range(PARTS):
        if j + 1 < PARTS:
            give(1, j + 1)
        upper[j] = take(1, j)
        ups.append(send(upper.at[j], above.at[j], up_sem, (j,), (after_g, b)))
    for j in range(PARTS):
        give(0, j)
    for j in range(PARTS):
        lower[j] = take(0, j)

    before_column = lax.shift_right_logical(before[0:1, :], 2)
    before_next = lax.rem(before_column + 1, n_band)

    def onto(n, j):
        shape = (lines, piece, length)
        value = jnp.where(column == n, lower[j, :, 0], 0.0) + jnp.where(next_column == n, lower[j, :, 1], 0.0)
        left = jnp.broadcast_to((before_column == n)[None], shape)
        right = jnp.broadcast_to((before_next == n)[None], shape)
        return value + jnp.where(left, above[j, :, 0], 0.0) + jnp.where(right, above[j, :, 1], 0.0)

    crossings = []

    def place(j):
        ups[j].wait_recv()
        row = []
        for i, o in enumerate(others):
            for e in range(2):
                to_chip[i, j, e] = onto(2 * o + e, j)
            row.append(send(to_chip.at[i, j], from_chip.at[i, j], row_sem, (i, j), (g, 2 * o + core)))
        crossings.append(row)
        for e in range(2):
            kept[j, e] = onto(2 * chip + e, j)

    endings = []

    def finish(j):
        own, given = kept[j, core], kept[j, 1 - core]
        for i, copy in enumerate(crossings[j]):
            copy.wait_recv()
            own = own + from_chip[i, j, core]
            given = given + from_chip[i, j, 1 - core]
        last[j] = given
        endings.append(send(last.at[j], ending.at[j], end_sem, (j,), pair))
        out_ref[pl.ds(share * core + lines * j, lines)] = own

    for j in range(PARTS):
        place(j)
        if j > 0:
            finish(j - 1)
    finish(PARTS - 1)
    for j in range(PARTS):
        endings[j].wait_recv()
        out_ref[pl.ds(share * (1 - core) + lines * j, lines)] = ending[j]
    for copy in sent:
        copy.wait_send()


def body(n_frag, n_band, wave_init, potential, fragment_order):
    slots, bands, depth, width, length = wave_init.shape
    assert slots == 1 and bands == 1 and n_band % 2 == 0
    slab, piece = potential.shape[:2]
    others = n_band // 2 - 1
    share = slab // 2
    lines = share // PARTS
    f32 = jnp.float32
    dma = pltpu.SemaphoreType.DMA
    part = (PARTS, lines, 2, piece, length)
    chip_part = (others, PARTS, 2, lines, piece, length)
    vmem = pl.BlockSpec(memory_space=pltpu.VMEM)
    return pl.pallas_call(
        functools.partial(kernel, n_frag, n_band, depth, width, length),
        out_shape=jax.ShapeDtypeStruct((slab, piece, length), f32),
        in_specs=[pl.BlockSpec(memory_space=pltpu.SMEM)] + [vmem] * 5,
        out_specs=vmem,
        scratch_shapes=[
            pltpu.VMEM((depth * width, length), f32),
            pltpu.VMEM((depth * width, length), f32),
            pltpu.VMEM((depth, 2, piece, length), f32),
            pltpu.VMEM((n_band, slab, piece, length), f32),
            pltpu.VMEM((PARTS, slab // PARTS, piece, length), f32),
            pltpu.VMEM((8, 128), jnp.int32),
            pltpu.VMEM((8, 128), jnp.int32),
            pltpu.VMEM((2, *part), f32),
            pltpu.VMEM((2, *part), f32),
            pltpu.VMEM(part, f32),
            pltpu.VMEM(part, f32),
            pltpu.VMEM(part, f32),
            pltpu.VMEM(chip_part, f32),
            pltpu.VMEM(chip_part, f32),
            pltpu.VMEM((PARTS, 2, lines, piece, length), f32),
            pltpu.VMEM((PARTS, lines, piece, length), f32),
            pltpu.VMEM((PARTS, lines, piece, length), f32),
            dma((2, 1)),
            dma((2, PARTS)),
            dma((2, others, PARTS)),
            dma((2, others, PARTS)),
            dma((2, PARTS)),
            dma((2, PARTS)),
            dma((2, 2, PARTS)),
            dma((2, PARTS)),
            dma((2, others, PARTS)),
            dma((2, PARTS)),
        ],
        compiler_params=pltpu.CompilerParams(
            collective_id=0, has_side_effects=True, vmem_limit_bytes=60 * 1024 * 1024
        ),
        name="fragment_step",
    )(
        fragment_order,
        wave_init.reshape(depth * width, length),
        potential,
        jnp.asarray(x_operator(length)),
        jnp.asarray(line_operators(depth)),
        jnp.asarray(line_operators(width)),
    )


def solution(mesh):
    placed = (P("frag", "band", None, None, None), P("frag", "band", None), P("frag", None))
    return jax.shard_map(
        functools.partial(body, mesh.shape["frag"], mesh.shape["band"]),
        mesh=mesh, in_specs=placed, out_specs=P("frag", "band", None), check_vma=False,
    )
```

```python
import functools

import jax
import jax.numpy as jnp
import numpy as np
from jax import lax
from jax.experimental import pallas as pl
from jax.experimental.pallas import tpu as pltpu
from jax.sharding import PartitionSpec as P

STEP_LENGTH = 0.1
EPSILON = 1e-06
MESH = pl.DeviceIdType.MESH
PARTS = 8
VMEM_BYTES = 40 * 1024 * 1024


def half_kinetic(extent, live_length):
    m = np.arange(live_length)
    weight = (2.0 * np.pi * np.minimum(m, live_length - m) / live_length) ** 2
    gap = m[:, None] - m[None, :]
    matrix = np.einsum(
        "m,mij->ij", weight, np.cos(2.0 * np.pi * (m[:, None, None] * gap[None] % live_length) / live_length)
    )
    full = np.zeros((extent, extent))
    full[:live_length, :live_length] = 0.5 * matrix / live_length
    return full


def two_parts(matrix):
    high = matrix.astype(jnp.bfloat16)
    low = (matrix - high.astype(np.float64)).astype(jnp.bfloat16)
    return high, low


def x_operator(length):
    high, low = two_parts(half_kinetic(length, length))
    return np.block([[high, low], [high, np.zeros_like(high)]]).astype(jnp.bfloat16)


def line_operators(extent, by_half):
    rows, halved = [], []
    for live in (extent // 2, extent):
        high, low = two_parts(half_kinetic(extent, live))
        rows.append(np.concatenate([high, low, high], axis=1))
        cut = extent // 2
        halved.append(np.concatenate(
            [part[:, own] for own in (slice(0, cut), slice(cut, extent)) for part in (high, low, high)], axis=1
        ))
    return np.stack(halved + rows if by_half else rows).astype(jnp.bfloat16)


def fold(block):
    return jnp.sum(block.reshape(-1, 8, block.shape[-1]), axis=0)


def dot(a, b):
    return jnp.dot(a, b, preferred_element_type=jnp.float32)


def split(block):
    high = block.astype(jnp.bfloat16)
    return high, (block - high.astype(jnp.float32)).astype(jnp.bfloat16)


def kernel(
    n_frag, n_band, depth, width, length,
    code_ref, wave_hbm, pot_ref, kx_hbm, kz_hbm, ky_hbm, out_ref,
    wave_ref, kx_ref, kz_ref, ky_ref, state, applied, twice, lifted, box, columns, picked, mine, before,
    to_pair, from_pair, upper, above, lower, to_chip, from_chip, kept, ending,
    load_sem, code_sem, pair_sem, chip_send, chip_recv, relay_sem, pick_sem, rise_sem,
    half_sem, up_sem, row_send, row_recv, end_sem,
):
    g = lax.axis_index("frag")
    b = lax.axis_index("band")
    core = lax.rem(b, 2)
    chip = lax.div(b, 2)
    chips = n_band // 2
    after_g = lax.rem(g + 1, n_frag)
    before_g = lax.rem(g + n_frag - 1, n_frag)
    pair = (g, chip * 2 + 1 - core)
    others = [lax.rem(chip + d, chips) for d in range(1, chips)]
    sources = [lax.rem(chip + chips - d, chips) for d in range(1, chips)]
    slab = depth // 2
    piece = width // 2
    share = slab // 2
    lines = share // PARTS
    sent = []

    def transfer(src, dst, send_sem, recv_sem, device):
        return pltpu.make_async_remote_copy(
            src_ref=src, dst_ref=dst, send_sem=send_sem, recv_sem=recv_sem,
            device_id=device, device_id_type=MESH,
        )

    def send(src, dst, sems, index, device):
        copy = transfer(src, dst, sems.at[(0, *index)], sems.at[(1, *index)], device)
        copy.start()
        sent.append(copy)
        return copy

    barrier = pltpu.get_barrier_semaphore()
    peers = [pair, (after_g, b), (before_g, b)] + [(g, 2 * o + e) for o in others for e in range(2)]
    for peer in peers:
        pl.semaphore_signal(barrier, inc=1, device_id=peer, device_id_type=MESH)
    loads = [
        pltpu.make_async_copy(src, dst, load_sem.at[n])
        for n, (src, dst) in enumerate((
            (wave_hbm, wave_ref), (kz_hbm, kz_ref), (kx_hbm, kx_ref), (ky_hbm, ky_ref), (pot_ref, columns.at[b])
        ))
    ]
    for load in loads:
        load.start()
    code = code_ref[0, 0]
    column = lax.shift_right_logical(code, 2)
    next_column = lax.rem(column + 1, n_band)
    z_double = lax.bitwise_and(lax.shift_right_logical(code, 1), 1)
    y_double = lax.bitwise_and(code, 1)
    mine[...] = jnp.full(mine.shape, code, jnp.int32)
    pl.semaphore_wait(barrier, len(peers))

    def slab_rows(half, j):
        return pl.ds(share * half + lines * j, lines)

    pair_copies = {}
    for j in range(PARTS):
        for i, o in enumerate(others):
            for e in range(2):
                rows = slab_rows(e, j)
                copy = transfer(
                    pot_ref.at[rows], columns.at[b, rows],
                    chip_send.at[i, e, j], chip_recv.at[i, core, j], (g, 2 * o + e),
                )
                copy.start()
                sent.append(copy)
        if j == 0:
            code_copy = send(mine, before, code_sem, (0,), (after_g, b))
        rows = slab_rows(1 - core, j)
        pair_copies[j] = send(pot_ref.at[rows], columns.at[b, rows], pair_sem, (0, j), pair)
    for j in range(PARTS):
        rows = slab_rows(core, j)
        pair_copies[PARTS + j] = send(pot_ref.at[rows], columns.at[b, rows], pair_sem, (1, j), pair)

    for load in loads[:2]:
        load.wait()
    y_live = lax.broadcasted_iota(jnp.int32, (width, length), 0) < piece * (1 + y_double)

    def begin(z, carry):
        rows = pl.ds(pl.multiple_of(z * width, width), width)
        live = jnp.logical_and(y_live, z < slab * (1 + z_double))
        state[rows, :] = jnp.where(live, wave_ref[rows, :].astype(jnp.float32), 0.0)
        return carry

    lax.fori_loop(0, depth, begin, 0, unroll=4)

    def first_z(first, count):
        op = kz_ref[2 + z_double][:, : 2 * depth]

        def one(i, carry):
            y = first + 2 * i
            parts = []
            for e in range(2):
                high = state[pl.ds(y + e, depth, stride=width), :].astype(jnp.bfloat16)
                parts.append(jnp.concatenate([high, high], axis=0))
            result = dot(op, jnp.concatenate(parts, axis=1))
            for e in range(2):
                applied[pl.ds(y + e, depth, stride=width), :] = result[:, e * length : (e + 1) * length]
            return carry

        lax.fori_loop(0, count // 2, one, 0, unroll=4)

    def two_rows(z):
        return pl.ds(pl.multiple_of(z * width, 2 * width), 2 * width)

    def first_xy(first, count):
        op = ky_ref[y_double][:, : 2 * width]

        def one(i, carry):
            rows = two_rows(first + 2 * i)
            high = state[rows, :].astype(jnp.bfloat16)
            wide = dot(high, kx_ref[0:length, :])
            parts = [jnp.concatenate([high[e * width : (e + 1) * width]] * 2, axis=0) for e in range(2)]
            tall = dot(op, jnp.concatenate(parts, axis=1))
            total = applied[rows, :] + (wide[:, :length] + wide[:, length:])
            applied[rows, :] = total + jnp.concatenate([tall[:, :length], tall[:, length:]], axis=0)
            return carry

        lax.fori_loop(0, count // 2, one, 0, unroll=4)

    picks, rises = [], []
    relays = []

    def pick_part(j):
        rows = slab_rows(core, j)
        pair_copies[j].wait_recv()
        for i, s in enumerate(sources):
            for e in range(2):
                here = columns.at[2 * s + e, rows]
                transfer(here, here, chip_send.at[i, e, j], chip_recv.at[i, e, j], pair).wait_recv()
        if j == 0:
            code_copy.wait_recv()
            loads[4].wait()
        base = lax.shift_right_logical(before[0:1, :], 2)
        for side in range(2):
            target = lax.rem(base + side, n_band)
            value = columns[0, rows]
            for n in range(1, n_band):
                value = jnp.where(jnp.broadcast_to((target == n)[None], value.shape), columns[n, rows], value)
            picked[j, :, side] = value
        place_at = pl.ds(slab + share * core + lines * j, lines)
        picks.append(send(picked.at[j], box.at[place_at], pick_sem, (j,), (before_g, b)))
        for i, s in enumerate(sources):
            for e in range(2):
                here = columns.at[2 * s + e, rows]
                relays.append(send(here, here, relay_sem, (i, e, j), pair))

    def pass_up(j):
        picks[j].wait_recv()
        here = box.at[pl.ds(slab + share * core + lines * j, lines)]
        rises.append(send(here, here, rise_sem, (j,), pair))

    quarter = width // 4
    first_z(0, quarter)
    first_z(quarter, quarter)
    pick_part(0)
    first_z(2 * quarter, quarter)
    first_z(3 * quarter, quarter)
    pick_part(1)
    loads[2].wait()
    loads[3].wait()
    quarter = depth // 4
    ready = 2
    for n in range(4):
        first_xy(n * quarter, quarter)
        pick_part(ready)
        ready += 1
        if n > 0:
            pass_up(n - 1)
    passed = 3
    while ready < PARTS:
        pick_part(ready)
        ready += 1
        pass_up(passed)
        passed += 1

    for j in range(PARTS):
        pair_copies[PARTS + j].wait_recv()
    for relay in relays:
        relay.wait_recv()

    def lower_box(z, carry):
        box[z, 0] = columns[column, z]
        box[z, 1] = columns[next_column, z]
        return carry

    lax.fori_loop(0, slab, lower_box, 0, unroll=4)

    def full_rows(z, sums):
        rows = two_rows(z)
        s = state[rows, :]
        v = box[pl.ds(z, 2)].reshape(2 * width, length)
        h = applied[rows, :] + v * s
        applied[rows, :] = h
        return (sums[0] + fold(s * s), sums[1] + fold(s * h), sums[2] + fold(h * h)), h, v

    def again_xy(z, h, v):
        rows = two_rows(z)
        high, low = split(h)
        wide = dot(jnp.concatenate([high, low], axis=1), kx_ref[...])
        parts = []
        for e in range(2):
            own = slice(e * width, (e + 1) * width)
            parts.append(jnp.concatenate([high[own], high[own], low[own]], axis=0))
        tall = dot(ky_ref[y_double], jnp.concatenate(parts, axis=1))
        total = v * h + (wide[:, :length] + wide[:, length:])
        twice[rows, :] = total + jnp.concatenate([tall[:, :length], tall[:, length:]], axis=0)

    def both(z, sums):
        sums, h, v = full_rows(z, sums)
        again_xy(z, h, v)
        return sums

    def z_parts(y, level):
        parts = []
        for e in range(2):
            high, low = split(applied[pl.ds(level * slab * width + y + e, slab, stride=width), :])
            parts.append(jnp.concatenate([high, high, low], axis=0))
        return jnp.concatenate(parts, axis=1)

    zero = jnp.zeros((8, length), jnp.float32)
    sums = (zero, zero, zero)
    while passed < PARTS:
        pass_up(passed)
        passed += 1
    sums = lax.fori_loop(0, slab // 2, lambda i, c: both(2 * i, c), sums, unroll=4)
    op = kz_ref[z_double]

    def low_z(i, carry):
        y = 2 * i
        result = dot(op[:, : 3 * slab], z_parts(y, 0))
        for e in range(2):
            lifted[pl.ds(y + e, depth, stride=width), :] = result[:, e * length : (e + 1) * length]
        return carry

    lax.fori_loop(0, width // 2, low_z, 0, unroll=4)
    for j in range(PARTS):
        for i in range(lines // 2):
            sums = both(slab + share * core + lines * j + 2 * i, sums)
    for j in range(PARTS):
        rises[j].wait_recv()
        for i in range(lines // 2):
            sums = both(slab + share * (1 - core) + lines * j + 2 * i, sums)

    def high_z(i, carry):
        cross, square = carry
        y = 2 * i
        result = dot(op[:, 3 * slab :], z_parts(y, 1))
        for e in range(2):
            at = pl.ds(y + e, depth, stride=width)
            total = twice[at, :] + lifted[at, :] + result[:, e * length : (e + 1) * length]
            twice[at, :] = total
            cross = cross + fold(applied[at, :] * total)
            square = square + fold(total * total)
        return cross, square

    cross, square = lax.fori_loop(0, width // 2, high_z, (zero, zero), unroll=4)

    def whole(block):
        return jnp.sum(block, axis=(0, 1), keepdims=True)

    ss, sh, hh = (whole(part) for part in sums)
    hb, bb = whole(cross), whole(square)
    tau = STEP_LENGTH
    a = 1.0 + tau * (sh / (ss + EPSILON))
    tt = a * a * ss - 2.0 * tau * a * sh + tau * tau * hh
    th = a * a * sh - 2.0 * tau * a * hh + tau * tau * hb
    qq = a * a * hh - 2.0 * tau * a * hb + tau * tau * bb
    cells = (slab * piece * length * (1 + z_double) * (1 + y_double)).astype(jnp.float32)
    scale1 = cells / (tt + EPSILON)
    a2 = 1.0 + tau * (scale1 * th / (scale1 * tt + EPSILON))
    uu = a2 * a2 * tt - 2.0 * tau * a2 * th + tau * tau * qq
    scale2 = cells / (scale1 * uu + EPSILON)
    sign = jnp.where(z_double == y_double, 1.0, -1.0).astype(jnp.float32) / n_band
    factor = sign * scale1 * scale2
    by_s, by_h, by_b = a2 * a, tau * (a2 + a), tau * tau

    def density(z):
        rows = pl.ds(pl.multiple_of(z * width, width), lines * width)
        u = by_s * state[rows, :] - by_h * applied[rows, :] + by_b * twice[rows, :]
        return (factor * (u * u)).reshape(lines, 2, piece, length)

    halves = {}

    def give(level, j):
        to_pair[level, j] = density(level * slab + share * (1 - core) + lines * j)
        halves[level, j] = send(to_pair.at[level, j], from_pair.at[level, j], half_sem, (level, j), pair)

    def take(level, j):
        own = density(level * slab + share * core + lines * j)
        halves[level, j].wait_recv()
        return own + from_pair[level, j]

    ups = []
    give(1, 0)
    give(1, 1)
    for j in range(PARTS):
        if j + 2 < PARTS:
            give(1, j + 2)
        upper[j] = take(1, j)
        ups.append(send(upper.at[j], above.at[j], up_sem, (j,), (after_g, b)))
    for j in range(PARTS):
        give(0, j)

    before_column = lax.shift_right_logical(before[0:1, :], 2)
    before_next = lax.rem(before_column + 1, n_band)

    def onto(n, j):
        shape = (lines, piece, length)
        value = jnp.where(column == n, lower[j, :, 0], 0.0) + jnp.where(next_column == n, lower[j, :, 1], 0.0)
        left = jnp.broadcast_to((before_column == n)[None], shape)
        right = jnp.broadcast_to((before_next == n)[None], shape)
        return value + jnp.where(left, above[j, :, 0], 0.0) + jnp.where(right, above[j, :, 1], 0.0)

    endings = []

    def place(j):
        lower[j] = take(0, j)
        ups[j].wait_recv()
        for i, o in enumerate(others):
            for e in range(2):
                to_chip[i, j, e] = onto(2 * o + e, j)
                copy = transfer(
                    to_chip.at[i, j, e], from_chip.at[i, core, j],
                    row_send.at[i, e, j], row_recv.at[i, core, j], (g, 2 * o + e),
                )
                copy.start()
                sent.append(copy)
        kept[0, j] = onto(2 * chip + 1 - core, j)
        endings.append(send(kept.at[0, j], ending.at[j], end_sem, (j,), pair))
        kept[1, j] = onto(b, j)

    def finish(j):
        endings[j].wait_recv()
        for half, own in ((core, kept[1, j]), (1 - core, ending[j])):
            for i in range(len(others)):
                here = from_chip.at[i, half, j]
                transfer(here, here, row_send.at[i, 0, j], row_recv.at[i, half, j], pair).wait_recv()
                own = own + from_chip[i, half, j]
            out_ref[slab_rows(half, j)] = own

    for j in range(PARTS):
        place(j)
        if j > 2:
            finish(j - 3)
    for j in range(PARTS - 3, PARTS):
        finish(j)
    for copy in sent:
        copy.wait_send()


def body(n_frag, n_band, wave_init, potential, fragment_order):
    slots, bands, depth, width, length = wave_init.shape
    assert slots == 1 and bands == 1 and n_band % 2 == 0
    slab, piece = potential.shape[:2]
    others = n_band // 2 - 1
    share = slab // 2
    lines = share // PARTS
    f32 = jnp.float32
    dma = pltpu.SemaphoreType.DMA
    part = (PARTS, lines, 2, piece, length)
    flat = (depth * width, length)
    column_part = (lines, piece, length)
    constants = (x_operator(length), line_operators(depth, True), line_operators(width, False))
    anywhere = pl.BlockSpec(memory_space=pltpu.HBM)
    return pl.pallas_call(
        functools.partial(kernel, n_frag, n_band, depth, width, length),
        out_shape=jax.ShapeDtypeStruct((slab, piece, length), f32),
        in_specs=[pl.BlockSpec(memory_space=pltpu.SMEM)] + [anywhere] * 5,
        out_specs=pl.BlockSpec(memory_space=pltpu.VMEM),
        scratch_shapes=[
            pltpu.VMEM(flat, jnp.bfloat16),
            *[pltpu.VMEM(constant.shape, jnp.bfloat16) for constant in constants],
            pltpu.VMEM(flat, f32),
            pltpu.VMEM(flat, f32),
            pltpu.VMEM(flat, f32),
            pltpu.VMEM(flat, f32),
            pltpu.VMEM((depth, 2, piece, length), f32),
            pltpu.VMEM((n_band, slab, piece, length), f32),
            pltpu.VMEM(part, f32),
            pltpu.VMEM((8, 128), jnp.int32),
            pltpu.VMEM((8, 128), jnp.int32),
            pltpu.VMEM((2, *part), f32),
            pltpu.VMEM((2, *part), f32),
            pltpu.VMEM(part, f32),
            pltpu.VMEM(part, f32),
            pltpu.VMEM(part, f32),
            pltpu.VMEM((others, PARTS, 2, *column_part), f32),
            pltpu.VMEM((others, 2, PARTS, *column_part), f32),
            pltpu.VMEM((2, PARTS, *column_part), f32),
            pltpu.VMEM((PARTS, *column_part), f32),
            dma((5,)),
            dma((2, 1)),
            dma((2, 2, PARTS)),
            dma((others, 2, PARTS)),
            dma((others, 2, PARTS)),
            dma((2, others, 2, PARTS)),
            dma((2, PARTS)),
            dma((2, PARTS)),
            dma((2, 2, PARTS)),
            dma((2, PARTS)),
            dma((others, 2, PARTS)),
            dma((others, 2, PARTS)),
            dma((2, PARTS)),
        ],
        compiler_params=pltpu.CompilerParams(
            collective_id=0, has_side_effects=True, vmem_limit_bytes=VMEM_BYTES
        ),
        name="fragment_step",
    )(
        fragment_order,
        wave_init.reshape(flat),
        potential,
        *[jnp.asarray(constant) for constant in constants],
    )


def solution(mesh):
    placed = (P("frag", "band", None, None, None), P("frag", "band", None), P("frag", None))
    return jax.shard_map(
        functools.partial(body, mesh.shape["frag"], mesh.shape["band"]),
        mesh=mesh, in_specs=placed, out_specs=P("frag", "band", None), check_vma=False,
    )
```

```python
import functools

import jax
import jax.numpy as jnp
import numpy as np
from jax import lax
from jax.experimental import pallas as pl
from jax.experimental.pallas import tpu as pltpu
from jax.sharding import PartitionSpec as P

STEP_LENGTH = 0.1
EPSILON = 1e-06
MESH = pl.DeviceIdType.MESH
PARTS = 8
PAD = 8
VMEM_BYTES = 62 * 1024 * 1024


def half_kinetic(extent, live_length):
    m = np.arange(live_length)
    weight = (2.0 * np.pi * np.minimum(m, live_length - m) / live_length) ** 2
    gap = m[:, None] - m[None, :]
    matrix = np.einsum(
        "m,mij->ij", weight, np.cos(2.0 * np.pi * (m[:, None, None] * gap[None] % live_length) / live_length)
    )
    full = np.zeros((extent, extent))
    full[:live_length, :live_length] = 0.5 * matrix / live_length
    return full


def two_parts(matrix):
    high = matrix.astype(jnp.bfloat16)
    low = (matrix - high.astype(np.float64)).astype(jnp.bfloat16)
    return high, low


def x_operator(length):
    high, low = two_parts(half_kinetic(length, length))
    return np.block([[high, low], [high, np.zeros_like(high)]]).astype(jnp.bfloat16)


def line_operators(extent):
    rows = []
    for live in (extent // 2, extent):
        high, low = two_parts(half_kinetic(extent, live))
        rows.append(np.concatenate([high, low, high], axis=1))
    return np.stack(rows).astype(jnp.bfloat16)


def fold(block):
    return jnp.sum(block.reshape(-1, 8, block.shape[-1]), axis=0)


def dot(a, b):
    return jnp.dot(a, b, preferred_element_type=jnp.float32)


def split(block):
    high = block.astype(jnp.bfloat16)
    return high, (block - high.astype(jnp.float32)).astype(jnp.bfloat16)


def kernel(
    n_frag, n_band, depth, width, length,
    code_ref, wave_hbm, pot_ref, kx_hbm, kz_hbm, ky_hbm, out_ref,
    wave_ref, kx_ref, kz_ref, ky_ref, state, applied, twice, box, columns, picked, mine, before,
    to_pair, from_pair, upper, above, lower, to_chip, from_chip, kept, ending,
    load_sem, code_sem, pair_sem, chip_send, chip_recv, relay_sem, pick_sem, rise_sem,
    half_sem, up_sem, row_send, row_recv, end_sem,
):
    g = lax.axis_index("frag")
    b = lax.axis_index("band")
    core = lax.rem(b, 2)
    chip = lax.div(b, 2)
    chips = n_band // 2
    after_g = lax.rem(g + 1, n_frag)
    before_g = lax.rem(g + n_frag - 1, n_frag)
    pair = (g, chip * 2 + 1 - core)
    others = [lax.rem(chip + d, chips) for d in range(1, chips)]
    sources = [lax.rem(chip + chips - d, chips) for d in range(1, chips)]
    slab = depth // 2
    piece = width // 2
    share = slab // 2
    lines = share // PARTS
    pitch = width + PAD
    sent = []

    def transfer(src, dst, send_sem, recv_sem, device):
        return pltpu.make_async_remote_copy(
            src_ref=src, dst_ref=dst, send_sem=send_sem, recv_sem=recv_sem,
            device_id=device, device_id_type=MESH,
        )

    def send(src, dst, sems, index, device):
        copy = transfer(src, dst, sems.at[(0, *index)], sems.at[(1, *index)], device)
        copy.start()
        sent.append(copy)
        return copy

    barrier = pltpu.get_barrier_semaphore()
    peers = [pair, (after_g, b), (before_g, b)] + [(g, 2 * o + e) for o in others for e in range(2)]
    for peer in peers:
        pl.semaphore_signal(barrier, inc=1, device_id=peer, device_id_type=MESH)
    loads = [
        pltpu.make_async_copy(src, dst, load_sem.at[n])
        for n, (src, dst) in enumerate((
            (wave_hbm, wave_ref), (kz_hbm, kz_ref), (kx_hbm, kx_ref), (ky_hbm, ky_ref), (pot_ref, columns.at[b])
        ))
    ]
    for load in loads:
        load.start()
    code = code_ref[0, 0]
    column = lax.shift_right_logical(code, 2)
    next_column = lax.rem(column + 1, n_band)
    z_double = lax.bitwise_and(lax.shift_right_logical(code, 1), 1)
    y_double = lax.bitwise_and(code, 1)
    mine[...] = jnp.full(mine.shape, code, jnp.int32)
    pl.semaphore_wait(barrier, len(peers))

    def slab_rows(half, j):
        return pl.ds(share * half + lines * j, lines)

    pair_copies = {}
    for j in range(PARTS):
        for i, o in enumerate(others):
            for e in range(2):
                rows = slab_rows(e, j)
                copy = transfer(
                    pot_ref.at[rows], columns.at[b, rows],
                    chip_send.at[i, e, j], chip_recv.at[i, core, j], (g, 2 * o + e),
                )
                copy.start()
                sent.append(copy)
        if j == 0:
            code_copy = send(mine, before, code_sem, (0,), (after_g, b))
        rows = slab_rows(1 - core, j)
        pair_copies[j] = send(pot_ref.at[rows], columns.at[b, rows], pair_sem, (0, j), pair)
    for j in range(PARTS):
        rows = slab_rows(core, j)
        pair_copies[PARTS + j] = send(pot_ref.at[rows], columns.at[b, rows], pair_sem, (1, j), pair)

    for load in loads[:2]:
        load.wait()
    y_live = lax.broadcasted_iota(jnp.int32, (width, length), 0) < piece * (1 + y_double)

    def begin(z, carry):
        rows = pl.ds(pl.multiple_of(z * width, width), width)
        live = jnp.logical_and(y_live, z < slab * (1 + z_double))
        state[pl.ds(pl.multiple_of(z * pitch, 8), width), :] = jnp.where(live, wave_ref[rows, :].astype(jnp.float32), 0.0)
        return carry

    lax.fori_loop(0, depth, begin, 0, unroll=4)

    def first_z(first, count):
        op = kz_ref[z_double][:, : 2 * depth]

        def one(i, carry):
            y = first + 2 * i
            parts = []
            for e in range(2):
                high = state[pl.ds(y + e, depth, stride=pitch), :].astype(jnp.bfloat16)
                parts.append(jnp.concatenate([high, high], axis=0))
            result = dot(op, jnp.concatenate(parts, axis=1))
            for e in range(2):
                applied[pl.ds(y + e, depth, stride=pitch), :] = result[:, e * length : (e + 1) * length]
            return carry

        lax.fori_loop(0, count // 2, one, 0, unroll=4)

    def lines_of(ref, z, count=2):
        return jnp.concatenate(
            [ref[pl.ds(pl.multiple_of((z + n) * pitch, 8), width), :] for n in range(count)], axis=0
        )

    def put_two(ref, z, value):
        for n in range(2):
            ref[pl.ds(pl.multiple_of((z + n) * pitch, 8), width), :] = value[n * width : (n + 1) * width]

    def first_xy(first, count):
        op = ky_ref[y_double][:, : 2 * width]

        def one(i, carry):
            z = first + 2 * i
            high = lines_of(state, z).astype(jnp.bfloat16)
            wide = dot(high, kx_ref[0:length, :])
            parts = [jnp.concatenate([high[e * width : (e + 1) * width]] * 2, axis=0) for e in range(2)]
            tall = dot(op, jnp.concatenate(parts, axis=1))
            total = lines_of(applied, z) + (wide[:, :length] + wide[:, length:])
            put_two(applied, z, total + jnp.concatenate([tall[:, :length], tall[:, length:]], axis=0))
            return carry

        lax.fori_loop(0, count // 2, one, 0, unroll=4)

    picks, rises = [], []
    relays = {}

    def pick_part(j):
        rows = slab_rows(core, j)
        pair_copies[j].wait_recv()
        for i, s in enumerate(sources):
            for e in range(2):
                here = columns.at[2 * s + e, rows]
                transfer(here, here, chip_send.at[i, e, j], chip_recv.at[i, e, j], pair).wait_recv()
        if j == 0:
            code_copy.wait_recv()
            loads[4].wait()
        base = lax.shift_right_logical(before[0:1, :], 2)
        for side in range(2):
            target = lax.rem(base + side, n_band)
            value = columns[0, rows]
            for n in range(1, n_band):
                value = jnp.where(jnp.broadcast_to((target == n)[None], value.shape), columns[n, rows], value)
            picked[j, :, side] = value
        place_at = pl.ds(slab + share * core + lines * j, lines)
        picks.append(send(picked.at[j], box.at[place_at], pick_sem, (j,), (before_g, b)))
        for i, s in enumerate(sources):
            for e in range(2):
                here = columns.at[2 * s + e, rows]
                relays[i, e, j] = send(here, here, relay_sem, (i, e, j), pair)

    def pass_up(j):
        picks[j].wait_recv()
        here = box.at[pl.ds(slab + share * core + lines * j, lines)]
        rises.append(send(here, here, rise_sem, (j,), pair))

    def full_rows(z, sums):
        s = lines_of(state, z)
        v = box[pl.ds(z, 2)].reshape(2 * width, length)
        h = lines_of(applied, z) + v * s
        put_two(applied, z, h)
        return (sums[0] + fold(s * s), sums[1] + fold(s * h), sums[2] + fold(h * h)), h, v

    def again_xy(z, h, v):
        high, low = split(h)
        wide = dot(jnp.concatenate([high, low], axis=1), kx_ref[...])
        parts = []
        for e in range(2):
            own = slice(e * width, (e + 1) * width)
            parts.append(jnp.concatenate([high[own], high[own], low[own]], axis=0))
        tall = dot(ky_ref[y_double], jnp.concatenate(parts, axis=1))
        total = v * h + (wide[:, :length] + wide[:, length:])
        put_two(twice, z, total + jnp.concatenate([tall[:, :length], tall[:, length:]], axis=0))

    def both(z, sums):
        sums, h, v = full_rows(z, sums)
        again_xy(z, h, v)
        return sums

    zero = jnp.zeros((8, length), jnp.float32)
    sums = (zero, zero, zero)
    def lower_part(j, sums):
        pair_copies[PARTS + j].wait_recv()
        for i in range(len(others)):
            for e in range(2):
                relays[i, e, j].wait_recv()
        for half in range(2):
            rows = slab_rows(half, j)
            for side, target in enumerate((column, next_column)):
                value = columns[0, rows]
                for n in range(1, n_band):
                    value = jnp.where(target == n, columns[n, rows], value)
                box[rows, side] = value
            for i in range(lines // 2):
                sums = both(share * half + lines * j + 2 * i, sums)
        return sums

    def upper_part(half, j, sums):
        for i in range(lines // 2):
            sums = both(slab + share * half + lines * j + 2 * i, sums)
        return sums

    quarter = width // 4
    first_z(0, quarter)
    first_z(quarter, quarter)
    pick_part(0)
    first_z(2 * quarter, quarter)
    first_z(3 * quarter, quarter)
    pick_part(1)
    loads[2].wait()
    loads[3].wait()
    quarter = depth // 4
    first_xy(0, quarter)
    first_xy(quarter, quarter)
    pick_part(2)
    first_xy(2 * quarter, quarter)
    pass_up(0)
    pick_part(3)
    first_xy(3 * quarter, quarter)
    for j in range(4, PARTS):
        sums = lower_part(j - 4, sums)
        pass_up(j - 3)
        pick_part(j)
    for j in range(PARTS - 4, PARTS):
        sums = lower_part(j, sums)
        if j == PARTS - 3:
            pass_up(PARTS - 3)
        if j == PARTS - 1:
            pass_up(PARTS - 2)
    pass_up(PARTS - 1)
    for j in range(PARTS):
        sums = upper_part(core, j, sums)
    for j in range(PARTS):
        rises[j].wait_recv()
        sums = upper_part(1 - core, j, sums)

    def again_z(i, carry):
        cross, square = carry
        at = [pl.ds(2 * i + e, depth, stride=pitch) for e in range(2)]
        lines_z = [applied[own, :] for own in at]
        parts = []
        for h in lines_z:
            high, low = split(h)
            parts.append(jnp.concatenate([high, high, low], axis=0))
        result = dot(kz_ref[z_double], jnp.concatenate(parts, axis=1))
        for e in range(2):
            total = twice[at[e], :] + result[:, e * length : (e + 1) * length]
            twice[at[e], :] = total
            cross = cross + fold(lines_z[e] * total)
            square = square + fold(total * total)
        return cross, square

    cross, square = lax.fori_loop(0, width // 2, again_z, (zero, zero), unroll=4)

    def whole(block):
        return jnp.sum(block, axis=(0, 1), keepdims=True)

    ss, sh, hh = (whole(part) for part in sums)
    hb, bb = whole(cross), whole(square)
    tau = STEP_LENGTH
    a = 1.0 + tau * (sh / (ss + EPSILON))
    tt = a * a * ss - 2.0 * tau * a * sh + tau * tau * hh
    th = a * a * sh - 2.0 * tau * a * hh + tau * tau * hb
    qq = a * a * hh - 2.0 * tau * a * hb + tau * tau * bb
    cells = (slab * piece * length * (1 + z_double) * (1 + y_double)).astype(jnp.float32)
    scale1 = cells / (tt + EPSILON)
    a2 = 1.0 + tau * (scale1 * th / (scale1 * tt + EPSILON))
    uu = a2 * a2 * tt - 2.0 * tau * a2 * th + tau * tau * qq
    scale2 = cells / (scale1 * uu + EPSILON)
    sign = jnp.where(z_double == y_double, 1.0, -1.0).astype(jnp.float32) / n_band
    factor = sign * scale1 * scale2
    by_s, by_h, by_b = a2 * a, tau * (a2 + a), tau * tau

    def density(z):
        u = by_s * lines_of(state, z, lines) - by_h * lines_of(applied, z, lines) + by_b * lines_of(twice, z, lines)
        return (factor * (u * u)).reshape(lines, 2, piece, length)

    halves = {}

    def give(level, j):
        to_pair[level, j] = density(level * slab + share * (1 - core) + lines * j)
        halves[level, j] = send(to_pair.at[level, j], from_pair.at[level, j], half_sem, (level, j), pair)

    def take(level, j):
        own = density(level * slab + share * core + lines * j)
        halves[level, j].wait_recv()
        return own + from_pair[level, j]

    ups = []
    give(1, 0)
    give(1, 1)
    for j in range(PARTS):
        if j + 2 < PARTS:
            give(1, j + 2)
        upper[j] = take(1, j)
        ups.append(send(upper.at[j], above.at[j], up_sem, (j,), (after_g, b)))
    for j in range(PARTS):
        give(0, j)

    before_column = lax.shift_right_logical(before[0:1, :], 2)
    before_next = lax.rem(before_column + 1, n_band)

    def onto(n, j):
        shape = (lines, piece, length)
        value = jnp.where(column == n, lower[j, :, 0], 0.0) + jnp.where(next_column == n, lower[j, :, 1], 0.0)
        left = jnp.broadcast_to((before_column == n)[None], shape)
        right = jnp.broadcast_to((before_next == n)[None], shape)
        return value + jnp.where(left, above[j, :, 0], 0.0) + jnp.where(right, above[j, :, 1], 0.0)

    endings = []

    def place(j):
        lower[j] = take(0, j)
        ups[j].wait_recv()
        for i, o in enumerate(others):
            for e in range(2):
                to_chip[i, j, e] = onto(2 * o + e, j)
                copy = transfer(
                    to_chip.at[i, j, e], from_chip.at[i, core, j],
                    row_send.at[i, e, j], row_recv.at[i, core, j], (g, 2 * o + e),
                )
                copy.start()
                sent.append(copy)
        kept[0, j] = onto(2 * chip + 1 - core, j)
        endings.append(send(kept.at[0, j], ending.at[j], end_sem, (j,), pair))
        kept[1, j] = onto(b, j)

    def finish(j):
        endings[j].wait_recv()
        for half, own in ((core, kept[1, j]), (1 - core, ending[j])):
            for i in range(len(others)):
                here = from_chip.at[i, half, j]
                transfer(here, here, row_send.at[i, 0, j], row_recv.at[i, half, j], pair).wait_recv()
                own = own + from_chip[i, half, j]
            out_ref[slab_rows(half, j)] = own

    for j in range(PARTS):
        place(j)
        if j > 2:
            finish(j - 3)
    for j in range(PARTS - 3, PARTS):
        finish(j)
    for copy in sent:
        copy.wait_send()


def body(n_frag, n_band, wave_init, potential, fragment_order):
    slots, bands, depth, width, length = wave_init.shape
    assert slots == 1 and bands == 1 and n_band % 2 == 0
    slab, piece = potential.shape[:2]
    others = n_band // 2 - 1
    share = slab // 2
    lines = share // PARTS
    f32 = jnp.float32
    dma = pltpu.SemaphoreType.DMA
    part = (PARTS, lines, 2, piece, length)
    flat = (depth * width, length)
    padded = (depth * (width + PAD), length)
    column_part = (lines, piece, length)
    constants = (x_operator(length), line_operators(depth), line_operators(width))
    anywhere = pl.BlockSpec(memory_space=pltpu.HBM)
    return pl.pallas_call(
        functools.partial(kernel, n_frag, n_band, depth, width, length),
        out_shape=jax.ShapeDtypeStruct((slab, piece, length), f32),
        in_specs=[pl.BlockSpec(memory_space=pltpu.SMEM)] + [anywhere] * 5,
        out_specs=pl.BlockSpec(memory_space=pltpu.VMEM),
        scratch_shapes=[
            pltpu.VMEM(flat, jnp.bfloat16),
            *[pltpu.VMEM(constant.shape, jnp.bfloat16) for constant in constants],
            pltpu.VMEM(padded, f32),
            pltpu.VMEM(padded, f32),
            pltpu.VMEM(padded, f32),
            pltpu.VMEM((depth, 2, piece, length), f32),
            pltpu.VMEM((n_band, slab, piece, length), f32),
            pltpu.VMEM(part, f32),
            pltpu.VMEM((8, 128), jnp.int32),
            pltpu.VMEM((8, 128), jnp.int32),
            pltpu.VMEM((2, *part), f32),
            pltpu.VMEM((2, *part), f32),
            pltpu.VMEM(part, f32),
            pltpu.VMEM(part, f32),
            pltpu.VMEM(part, f32),
            pltpu.VMEM((others, PARTS, 2, *column_part), f32),
            pltpu.VMEM((others, 2, PARTS, *column_part), f32),
            pltpu.VMEM((2, PARTS, *column_part), f32),
            pltpu.VMEM((PARTS, *column_part), f32),
            dma((5,)),
            dma((2, 1)),
            dma((2, 2, PARTS)),
            dma((others, 2, PARTS)),
            dma((others, 2, PARTS)),
            dma((2, others, 2, PARTS)),
            dma((2, PARTS)),
            dma((2, PARTS)),
            dma((2, 2, PARTS)),
            dma((2, PARTS)),
            dma((others, 2, PARTS)),
            dma((others, 2, PARTS)),
            dma((2, PARTS)),
        ],
        compiler_params=pltpu.CompilerParams(
            collective_id=0, has_side_effects=True, vmem_limit_bytes=VMEM_BYTES
        ),
        name="fragment_step",
    )(
        fragment_order,
        wave_init.reshape(flat),
        potential,
        *[jnp.asarray(constant) for constant in constants],
    )


def solution(mesh):
    placed = (P("frag", "band", None, None, None), P("frag", "band", None), P("frag", None))
    return jax.shard_map(
        functools.partial(body, mesh.shape["frag"], mesh.shape["band"]),
        mesh=mesh, in_specs=placed, out_specs=P("frag", "band", None), check_vma=False,
    )
```
